32 devices in a mesh: seq: 16 (over z, x, core), head: 2 (over y).
Axes of the slice: x: 2, y: 2, z: 4, core: 2. Of those that a mesh axis runs over, the one named last changes fastest.
Arguments:
- packed_inputs_slab: bfloat16 [2048, 4096], P(('seq', 'head')), may hold values from -6 to 6
- lagged_blend_coefs: float32 [5, 4096], replicated, may hold values from 0 to 1
- acceptor_projector: bfloat16 [4096, 4096], P('seq', 'head'), may hold values from -0.09375 to 0.09375
- address_projector: bfloat16 [4096, 4096], P('seq', 'head'), may hold values from -0.09375 to 0.09375
- payload_projector: bfloat16 [4096, 4096], P('seq', 'head'), may hold values from -0.09375 to 0.09375
- fading_offset_entry: float32 [4096], P('head'), may hold values from -12 to -2
- fading_left_matrix: bfloat16 [4096, 128], replicated, may hold values from -0.09375 to 0.09375
- fading_right_matrix: bfloat16 [128, 4096], P(None, 'head'), may hold values from -0.5 to 0.5
- learning_rate_offset: float32 [4096], P('head'), may hold values from -4 to 4
- learning_left_matrix: bfloat16 [4096, 128], replicated, may hold values from -0.09375 to 0.09375
- learning_right_matrix: bfloat16 [128, 4096], P(None, 'head'), may hold values from -0.5 to 0.5
- address_before_unitize: float32 [4096], P('head'), may hold values from 0.5 to 1.5
- address_learning_strength: float32 [4096], P('head'), may hold values from 0.5 to 1.5
- extra_reward_coefs: float32 [4096], P('head'), may hold values from -0.6 to 0.6
- cluster_normalize_multiplier: float32 [4096], P('head'), may hold values from 0.5 to 1.5
- paper_spans_sizes: int32 [4], replicated, may hold values from 1 to 16, 32 in all
Outputs:
- time_mixed: bfloat16 [2048, 4096], P('seq', 'head')
The draws below stay inside these ranges and needn't reach their ends.
Inputs may be any that keep to these rules, and one draw needn't show every extreme that they name: `paper_spans_sizes`: the lengths sum to 32 and the longest is exactly 16.
All inputs are finite; a program needn't handle non-finite values.
Results may differ from the reference program's by a relative error of at most 0.0077.
Values may be sent and summed in bfloat16 or wider, within the bound.
A program may use at most 128 MiB of HBM per device.

```python
import math
import jax
import jax.numpy as jnp
import numpy as np
from jax import lax

EMBED_DIMENSION = 4096
LANE_FEATURES = 64
DECAY_RANK = 128
ICL_RANK = 128
SPAN = 64
TOKENS = 2048
SPANS = 32
MOST_CH = 16
DOCS = 4


def draw_fading_offset_entry(key, part):
    head_key, fast_key, slow_key = jax.random.split(jax.random.fold_in(key, 17), 3)
    fast_share = 0.5
    fast_heads = jax.random.uniform(head_key, (EMBED_DIMENSION // LANE_FEATURES,), jnp.float32) < fast_share
    fast_values = jax.random.uniform(fast_key, (EMBED_DIMENSION,), jnp.float32, -4.0, -2.0)
    slow_values = jax.random.uniform(slow_key, (EMBED_DIMENSION,), jnp.float32, -12.0, -10.0)
    channel_head = jnp.arange(EMBED_DIMENSION) // LANE_FEATURES
    return jnp.where(fast_heads[channel_head], fast_values, slow_values).astype(jnp.float32)


def levels(key, shape, shards, low, top_value):
    gain = 1.0
    for position, blocks in shards:
        steps = jax.random.uniform(jax.random.fold_in(jax.random.fold_in(key, 6), position), (blocks,), jnp.float32, low / len(shards), top_value / len(shards))
        gain = gain * jnp.repeat(jnp.exp(steps), shape[position] // blocks).reshape((-1,) + (1,) * (len(shape) - 1 - position))
    return gain


def length_profile(amount, total, bound, slope):
    portions = [(1 << 20) // math.isqrt(rank ** slope) + 1 for rank in range(2, amount + 1)]
    rest, given = total - bound - (amount - 1), [1] * (amount - 1)
    while rest > 0:
        movable = [i for i in range(amount - 1) if given[i] < bound]
        pool, remaining = sum([portions[i] for i in movable]), rest
        for i in movable:
            more = min(bound - given[i], max(1, remaining * portions[i] // pool), rest)
            given[i] = given[i] + more
            rest = rest - more
    return np.array([bound] + given)


def ragged_sizes(key, count, total, bound, lean):
    if count == 2:
        one = jax.random.randint(key, (), max(1, total - bound), min(bound, total - 1) + 1)
        return jnp.stack([one, total - one])
    lengths = jnp.asarray(length_profile(count, total, bound, lean), jnp.int32)
    twos = (count - 1) // 2
    donor, taker = lengths[1:1 + 2 * twos:2], lengths[2:2 + 2 * twos:2]
    room = jnp.minimum(donor - 1, bound - taker)
    moved = jax.random.randint(jax.random.fold_in(key, 1), (twos,), 0, 1 << 20) % (room + 1)
    lengths = lengths.at[1:1 + 2 * twos:2].set(donor - moved).at[2:2 + 2 * twos:2].set(taker + moved)
    return lengths[jax.random.permutation(jax.random.fold_in(key, 2), count)]


def bell_draw(rng, extent, scale, bound, cuts=(), held_as=jnp.bfloat16):
    loudness = levels(rng, extent, cuts, -0.22, 0.18) if cuts else 1.0
    values = jax.random.normal(rng, extent, jnp.float32) * scale * loudness
    return jnp.minimum(jnp.maximum(values, -bound), bound).astype(held_as)


def setup_inputs(seed: int = 0) -> dict:
    keys = jax.random.split(jax.random.key(seed), 17)
    packed_inputs_slab = bell_draw(keys[0], (TOKENS, EMBED_DIMENSION), 1.0, 6.0, ((0, 32),))
    lagged_blend_coefs = jnp.clip(jax.random.uniform(keys[1], (5, EMBED_DIMENSION), jnp.float32, 0.0, 1.0), 0.0, 1.0)
    acceptor_projector = bell_draw(keys[2], (EMBED_DIMENSION, EMBED_DIMENSION), EMBED_DIMENSION ** -0.5, 0.09375, ((0, 16), (1, 2)))
    address_projector = bell_draw(keys[3], (EMBED_DIMENSION, EMBED_DIMENSION), EMBED_DIMENSION ** -0.5, 0.09375, ((0, 16), (1, 2)))
    payload_projector = bell_draw(keys[4], (EMBED_DIMENSION, EMBED_DIMENSION), EMBED_DIMENSION ** -0.5, 0.09375, ((0, 16), (1, 2)))
    fading_offset_entry = draw_fading_offset_entry(jax.random.fold_in(keys[16], 71), 0)
    fading_left_matrix = bell_draw(keys[6], (EMBED_DIMENSION, DECAY_RANK), EMBED_DIMENSION ** -0.5, 0.09375)
    fading_right_matrix = bell_draw(keys[7], (DECAY_RANK, EMBED_DIMENSION), DECAY_RANK ** -0.5, 0.5, ((1, 2),))
    learning_rate_offset = bell_draw(keys[8], (EMBED_DIMENSION,), 1.0, 4.0, ((0, 2),), jnp.float32)
    learning_left_matrix = bell_draw(keys[9], (EMBED_DIMENSION, ICL_RANK), EMBED_DIMENSION ** -0.5, 0.09375)
    learning_right_matrix = bell_draw(keys[10], (ICL_RANK, EMBED_DIMENSION), ICL_RANK ** -0.5, 0.5, ((1, 2),))
    address_before_unitize = jnp.clip(1.0 + 0.1 * jax.random.normal(keys[11], (EMBED_DIMENSION,), jnp.float32), 0.5, 1.5)
    address_learning_strength = jnp.clip(1.0 + 0.1 * jax.random.normal(keys[12], (EMBED_DIMENSION,), jnp.float32), 0.5, 1.5)
    extra_reward_coefs = bell_draw(keys[13], (EMBED_DIMENSION,), 0.1, 0.6, ((0, 2),), jnp.float32)
    cluster_normalize_multiplier = jnp.clip(1.0 + 0.1 * jax.random.normal(keys[14], (EMBED_DIMENSION,), jnp.float32), 0.5, 1.5)
    paper_spans_sizes = ragged_sizes(keys[15], DOCS, SPANS, MOST_CH, 2).astype(jnp.int32)
    return {"packed_inputs_slab": packed_inputs_slab, "lagged_blend_coefs": lagged_blend_coefs, "acceptor_projector": acceptor_projector, "address_projector": address_projector, "payload_projector": payload_projector, "fading_offset_entry": fading_offset_entry, "fading_left_matrix": fading_left_matrix, "fading_right_matrix": fading_right_matrix, "learning_rate_offset": learning_rate_offset, "learning_left_matrix": learning_left_matrix, "learning_right_matrix": learning_right_matrix, "address_before_unitize": address_before_unitize, "address_learning_strength": address_learning_strength, "extra_reward_coefs": extra_reward_coefs, "cluster_normalize_multiplier": cluster_normalize_multiplier, "paper_spans_sizes": paper_spans_sizes}


exact_precision = lax.Precision.HIGHEST
norm_eps = 1e-05
decay_limit = 0.606531

def product(left, right):
    return jnp.matmul(left, right, precision=exact_precision)

def flipped(matrix):
    return jnp.swapaxes(matrix, -1, -2)

def mixed_inputs(packed_inputs_slab, earlier, lagged_blend_coefs):
    current = packed_inputs_slab.astype(jnp.float32)
    change = earlier.astype(jnp.float32) - current
    return [(current + change * lagged_blend_coefs[member]).astype(jnp.bfloat16) for member in range(5)]

def prepare(acceptor_lines, keyed, payload_entries, x_decay, x_icl, fading_offset_entry, fading_left_matrix, fading_right_matrix, learning_rate_offset, learning_left_matrix, learning_right_matrix, address_before_unitize, address_learning_strength):
    decay_low = jnp.tanh(jnp.dot(x_decay.astype(jnp.float32), fading_left_matrix.astype(jnp.float32), preferred_element_type=jnp.float32)).astype(jnp.bfloat16)
    log_decay = -decay_limit * jax.nn.sigmoid(fading_offset_entry + jnp.dot(decay_low.astype(jnp.float32), fading_right_matrix.astype(jnp.float32), preferred_element_type=jnp.float32))
    icl_low = jnp.dot(x_icl.astype(jnp.float32), learning_left_matrix.astype(jnp.float32), preferred_element_type=jnp.float32).astype(jnp.bfloat16)
    icl = jax.nn.sigmoid(learning_rate_offset + jnp.dot(icl_low.astype(jnp.float32), learning_right_matrix.astype(jnp.float32), preferred_element_type=jnp.float32))
    row_count = acceptor_lines.shape[0]
    attention_lane_count = acceptor_lines.shape[1] // LANE_FEATURES
    head_shape = (row_count, attention_lane_count, LANE_FEATURES)
    scaled = (keyed * address_before_unitize).reshape(head_shape)
    unit_key = scaled / jnp.sqrt(lax.optimization_barrier(jnp.sum(scaled * scaled, axis=-1, keepdims=True)) + norm_eps)
    icl_heads = icl.reshape(head_shape)
    adjusted_address = keyed.reshape(head_shape) * (1.0 + (icl_heads - 1.0) * address_learning_strength.reshape(attention_lane_count, LANE_FEATURES))
    return (acceptor_lines.reshape(head_shape), adjusted_address, payload_entries.reshape(head_shape), log_decay.reshape(head_shape), -unit_key, unit_key * icl_heads)

def ending_result(result_lines, acceptor_lines, adjusted_address, payload_entries, extra_reward_coefs, cluster_normalize_multiplier):
    attention_lane_count = result_lines.shape[1]
    average = lax.optimization_barrier(jnp.mean(result_lines, axis=-1, keepdims=True))
    centered = result_lines - average
    spread = lax.optimization_barrier(jnp.mean(centered * centered, axis=-1, keepdims=True))
    unitized_result = centered / jnp.sqrt(spread + norm_eps) * cluster_normalize_multiplier.reshape(attention_lane_count, LANE_FEATURES)
    present_reward = lax.optimization_barrier(jnp.sum(acceptor_lines * adjusted_address * extra_reward_coefs.reshape(attention_lane_count, LANE_FEATURES), axis=-1, keepdims=True)) * payload_entries
    return (unitized_result + present_reward).reshape(result_lines.shape[0], -1).astype(jnp.bfloat16)

def span_terms(log_decay, acceptor_lines, keyed, alpha, beta):
    length = log_decay.shape[-2]
    log_sums = jnp.cumsum(log_decay, axis=-2)
    decay_in = jnp.exp(log_sums)
    decay_before = jnp.exp(log_sums - log_decay)
    inverse = jnp.exp(-log_sums)
    decay_out = jnp.exp(log_sums[..., -1:, :] - log_sums)
    alpha_dec = alpha * decay_before
    recept_dec = acceptor_lines * decay_in
    beta_inv = beta * inverse
    key_inv = keyed * inverse
    row_index = lax.broadcasted_iota(jnp.int32, (length, length), 0)
    col_index = lax.broadcasted_iota(jnp.int32, (length, length), 1)
    strict = row_index > col_index
    on_or_below = row_index >= col_index
    solve_matrix = jnp.eye(length, dtype=jnp.float32) - jnp.where(strict, product(alpha_dec, flipped(beta_inv)), 0.0)
    key_read = jnp.where(strict, product(alpha_dec, flipped(key_inv)), 0.0)
    out_beta = jnp.where(on_or_below, product(recept_dec, flipped(beta_inv)), 0.0)
    out_key = jnp.where(on_or_below, product(recept_dec, flipped(key_inv)), 0.0)
    return (solve_matrix, key_read, out_beta, out_key, alpha_dec, recept_dec, decay_in[..., -1, :], decay_out)

def recurrence(acceptor_lines, keyed, payload_entries, log_decay, alpha, beta, resets):
    attention_lane_count = acceptor_lines.shape[1]

    def blocks(array):
        return array.reshape(SPANS, SPAN, attention_lane_count, LANE_FEATURES)

    def step(carried, inputs):
        arrays = [jnp.swapaxes(array, 0, 1) for array in inputs[:6]]
        recept_c, key_c, value_c, decay_c, alpha_c, beta_c = arrays
        carried = carried * (1.0 - inputs[6])
        solve_matrix, key_read, out_beta, out_key, alpha_dec, recept_dec, decay_last, decay_out = span_terms(decay_c, recept_c, key_c, alpha_c, beta_c)
        right_side = product(alpha_dec, flipped(carried)) + product(key_read, value_c)
        reads = jax.scipy.linalg.solve_triangular(solve_matrix, right_side, lower=True, unit_diagonal=True)
        result_lines = product(recept_dec, flipped(carried)) + product(out_beta, reads) + product(out_key, value_c)
        updated = carried * decay_last[:, None, :] + product(flipped(reads), beta_c * decay_out) + product(flipped(value_c), key_c * decay_out)
        return (updated, jnp.swapaxes(result_lines, 0, 1))
    initial = jnp.zeros((attention_lane_count, LANE_FEATURES, LANE_FEATURES), jnp.float32)
    sequence = (blocks(acceptor_lines), blocks(keyed), blocks(payload_entries), blocks(log_decay), blocks(alpha), blocks(beta), resets.astype(jnp.float32))
    final_state, result_lines = lax.scan(step, initial, sequence)
    return result_lines.reshape(SPANS * SPAN, attention_lane_count, LANE_FEATURES)

def reference(packed_inputs_slab, lagged_blend_coefs, acceptor_projector, address_projector, payload_projector, fading_offset_entry, fading_left_matrix, fading_right_matrix, learning_rate_offset, learning_left_matrix, learning_right_matrix, address_before_unitize, address_learning_strength, extra_reward_coefs, cluster_normalize_multiplier, paper_spans_sizes):
    row_count = packed_inputs_slab.shape[0]
    doc_starts = jnp.cumsum(paper_spans_sizes) - paper_spans_sizes
    span_ids = jnp.arange(SPANS, dtype=jnp.int32)
    resets = jnp.any(doc_starts[None, :] == span_ids[:, None], axis=1)
    row_start = jnp.logical_and(jnp.arange(row_count) % SPAN == 0, jnp.repeat(resets, SPAN))
    earlier = jnp.concatenate([jnp.zeros((1, packed_inputs_slab.shape[1]), jnp.bfloat16), packed_inputs_slab[:-1]], axis=0)
    earlier = jnp.where(row_start[:, None], jnp.zeros_like(earlier), earlier)
    x_recept, x_decay, x_key, x_value, x_icl = mixed_inputs(packed_inputs_slab, earlier, lagged_blend_coefs)
    acceptor_lines = jnp.dot(x_recept.astype(jnp.float32), acceptor_projector.astype(jnp.float32), preferred_element_type=jnp.float32)
    keyed = jnp.dot(x_key.astype(jnp.float32), address_projector.astype(jnp.float32), preferred_element_type=jnp.float32)
    payload_entries = jnp.dot(x_value.astype(jnp.float32), payload_projector.astype(jnp.float32), preferred_element_type=jnp.float32)
    acceptor_lines, adjusted_address, payload_entries, log_decay, alpha, beta = prepare(acceptor_lines, keyed, payload_entries, x_decay, x_icl, fading_offset_entry, fading_left_matrix, fading_right_matrix, learning_rate_offset, learning_left_matrix, learning_right_matrix, address_before_unitize, address_learning_strength)
    result_lines = recurrence(acceptor_lines, adjusted_address, payload_entries, log_decay, alpha, beta, resets)
    return ending_result(result_lines, acceptor_lines, adjusted_address, payload_entries, extra_reward_coefs, cluster_normalize_multiplier)
```

```python
import functools

import jax
import jax.numpy as jnp
from jax import lax
from jax.experimental import pallas as pl
from jax.experimental.pallas import tpu as pltpu
from jax.sharding import PartitionSpec as P

LANE_FEATURES = 64
SPAN = 64


exact_precision = lax.Precision.HIGHEST
norm_eps = 1e-05
decay_limit = 0.606531


def passed_along(block, axis, distance):
    devices = range(lax.axis_size(axis))
    route = [(i - distance, i) for i in devices if i - distance in devices]
    return lax.ppermute(block, axis, route)


def product(left, right):
    return jnp.matmul(left, right, precision=exact_precision)


def flipped(matrix):
    return jnp.swapaxes(matrix, -1, -2)


def mixed_inputs(packed_inputs_slab, earlier, lagged_blend_coefs):
    current = packed_inputs_slab.astype(jnp.float32)
    change = earlier.astype(jnp.float32) - current
    return [
        (current + change * lagged_blend_coefs[member]).astype(jnp.bfloat16) for member in range(5)
    ]


def prepare(
    acceptor_lines,
    keyed,
    payload_entries,
    x_decay,
    x_icl,
    fading_offset_entry,
    fading_left_matrix,
    fading_right_matrix,
    learning_rate_offset,
    learning_left_matrix,
    learning_right_matrix,
    address_before_unitize,
    address_learning_strength,
):
    decay_low = jnp.tanh(
        jnp.dot(x_decay, fading_left_matrix, preferred_element_type=jnp.float32)
    ).astype(jnp.bfloat16)
    log_decay = -decay_limit * jax.nn.sigmoid(
        fading_offset_entry
        + jnp.dot(decay_low, fading_right_matrix, preferred_element_type=jnp.float32)
    )
    icl_low = jnp.dot(x_icl, learning_left_matrix, preferred_element_type=jnp.float32).astype(
        jnp.bfloat16
    )
    icl = jax.nn.sigmoid(
        learning_rate_offset
        + jnp.dot(icl_low, learning_right_matrix, preferred_element_type=jnp.float32)
    )
    row_count = acceptor_lines.shape[0]
    attention_lane_count = acceptor_lines.shape[1] // LANE_FEATURES
    head_shape = (row_count, attention_lane_count, LANE_FEATURES)
    scaled = (keyed * address_before_unitize).reshape(head_shape)
    unit_key = scaled / jnp.sqrt(jnp.sum(scaled * scaled, axis=-1, keepdims=True) + norm_eps)
    icl_heads = icl.reshape(head_shape)
    adjusted_address = keyed.reshape(head_shape) * (
        1.0
        + (icl_heads - 1.0) * address_learning_strength.reshape(attention_lane_count, LANE_FEATURES)
    )
    return (
        acceptor_lines.reshape(head_shape),
        adjusted_address,
        payload_entries.reshape(head_shape),
        log_decay.reshape(head_shape),
        -unit_key,
        unit_key * icl_heads,
    )


def ending_result(
    result_lines,
    acceptor_lines,
    adjusted_address,
    payload_entries,
    extra_reward_coefs,
    cluster_normalize_multiplier,
):
    attention_lane_count = result_lines.shape[1]
    average = jnp.mean(result_lines, axis=-1, keepdims=True)
    centered = result_lines - average
    spread = jnp.mean(centered * centered, axis=-1, keepdims=True)
    unitized_result = (
        centered
        / jnp.sqrt(spread + norm_eps)
        * cluster_normalize_multiplier.reshape(attention_lane_count, LANE_FEATURES)
    )
    present_reward = (
        jnp.sum(
            acceptor_lines
            * adjusted_address
            * extra_reward_coefs.reshape(attention_lane_count, LANE_FEATURES),
            axis=-1,
            keepdims=True,
        )
        * payload_entries
    )
    return (
        (unitized_result + present_reward).reshape(result_lines.shape[0], -1).astype(jnp.bfloat16)
    )


def span_terms(log_decay, acceptor_lines, keyed, alpha, beta):
    length = log_decay.shape[-2]
    log_sums = jnp.cumsum(log_decay, axis=-2)
    decay_in = jnp.exp(log_sums)
    decay_before = jnp.exp(log_sums - log_decay)
    inverse = jnp.exp(-log_sums)
    decay_out = jnp.exp(log_sums[..., -1:, :] - log_sums)
    alpha_dec = alpha * decay_before
    recept_dec = acceptor_lines * decay_in
    beta_inv = beta * inverse
    key_inv = keyed * inverse
    row_index = lax.broadcasted_iota(jnp.int32, (length, length), 0)
    col_index = lax.broadcasted_iota(jnp.int32, (length, length), 1)
    strict = row_index > col_index
    on_or_below = row_index >= col_index
    solve_matrix = jnp.eye(length, dtype=jnp.float32) - jnp.where(
        strict, product(alpha_dec, flipped(beta_inv)), 0.0
    )
    key_read = jnp.where(strict, product(alpha_dec, flipped(key_inv)), 0.0)
    out_beta = jnp.where(on_or_below, product(recept_dec, flipped(beta_inv)), 0.0)
    out_key = jnp.where(on_or_below, product(recept_dec, flipped(key_inv)), 0.0)
    return (
        solve_matrix,
        key_read,
        out_beta,
        out_key,
        alpha_dec,
        recept_dec,
        decay_in[..., -1, :],
        decay_out,
    )


def per_device(
    packed_inputs_slab,
    lagged_blend_coefs,
    acceptor_projector,
    address_projector,
    payload_projector,
    fading_offset_entry,
    fading_left_matrix,
    fading_right_matrix,
    learning_rate_offset,
    learning_left_matrix,
    learning_right_matrix,
    address_before_unitize,
    address_learning_strength,
    extra_reward_coefs,
    cluster_normalize_multiplier,
    paper_spans_sizes,
):
    gathered = lax.all_gather(packed_inputs_slab, "head", axis=0, tiled=True)
    row_count = gathered.shape[0]
    block_count = row_count // SPAN
    doc_starts = jnp.cumsum(paper_spans_sizes) - paper_spans_sizes
    span_ids = lax.axis_index("seq") * block_count + jnp.arange(block_count, dtype=jnp.int32)
    resets = jnp.any(doc_starts[None, :] == span_ids[:, None], axis=1)
    edge_token = passed_along(gathered[-1:], "seq", 1)
    earlier = jnp.concatenate([edge_token, gathered[:-1]], axis=0)
    row_start = jnp.logical_and(jnp.arange(row_count) % SPAN == 0, jnp.repeat(resets, SPAN))
    earlier = jnp.where(row_start[:, None], jnp.zeros_like(earlier), earlier)
    x_recept, x_decay, x_key, x_value, x_icl = mixed_inputs(gathered, earlier, lagged_blend_coefs)
    whole_recept = lax.all_gather(acceptor_projector, "seq", axis=0, tiled=True)
    whole_key = lax.all_gather(address_projector, "seq", axis=0, tiled=True)
    whole_value = lax.all_gather(payload_projector, "seq", axis=0, tiled=True)
    acceptor_lines = jnp.dot(x_recept, whole_recept, preferred_element_type=jnp.float32)
    keyed = jnp.dot(x_key, whole_key, preferred_element_type=jnp.float32)
    payload_entries = jnp.dot(x_value, whole_value, preferred_element_type=jnp.float32)
    acceptor_lines, adjusted_address, payload_entries, log_decay, alpha, beta = prepare(
        acceptor_lines,
        keyed,
        payload_entries,
        x_decay,
        x_icl,
        fading_offset_entry,
        fading_left_matrix,
        fading_right_matrix,
        learning_rate_offset,
        learning_left_matrix,
        learning_right_matrix,
        address_before_unitize,
        address_learning_strength,
    )
    attention_lane_count = acceptor_lines.shape[1]

    def blocks(array):
        return jnp.swapaxes(
            array.reshape(block_count, SPAN, attention_lane_count, LANE_FEATURES), 1, 2
        )

    recept_b, key_b, value_b, decay_b, alpha_b, beta_b = [
        blocks(array)
        for array in (acceptor_lines, adjusted_address, payload_entries, log_decay, alpha, beta)
    ]
    solve_matrix, key_read, out_beta, out_key, alpha_dec, recept_dec, decay_last, decay_out = (
        span_terms(decay_b, recept_b, key_b, alpha_b, beta_b)
    )
    right_side = jnp.concatenate([alpha_dec, product(key_read, value_b)], axis=-1)
    solved = jax.scipy.linalg.solve_triangular(
        solve_matrix, right_side, lower=True, unit_diagonal=True
    )
    linear_reads = solved[..., :LANE_FEATURES]
    offset_reads = solved[..., LANE_FEATURES:]
    queries = recept_dec + product(out_beta, linear_reads)
    output_base = product(out_beta, offset_reads) + product(out_key, value_b)
    beta_out = beta_b * decay_out
    identity = jnp.eye(LANE_FEATURES, dtype=jnp.float32)
    step_map = identity * decay_last[..., None, :] + product(flipped(linear_reads), beta_out)
    step_add = product(flipped(offset_reads), beta_out) + product(
        flipped(value_b), key_b * decay_out
    )
    carry_keep = 1.0 - resets.astype(jnp.float32)
    device_map = jnp.broadcast_to(identity, (attention_lane_count, LANE_FEATURES, LANE_FEATURES))
    device_add = jnp.zeros((attention_lane_count, LANE_FEATURES, LANE_FEATURES), jnp.float32)
    for position in range(block_count):
        masked = step_map[position] * carry_keep[position]
        device_map = product(device_map, masked)
        device_add = product(device_add, masked) + step_add[position]
    seq_count = lax.axis_size("seq")
    longest = seq_count * block_count // 2
    rounds = min(seq_count - 1, (longest + block_count - 2) // block_count)

    def advance(rounds_done, arriving):
        leaving = product(arriving, device_map) + device_add
        return passed_along(leaving, "seq", 1)

    incoming = lax.fori_loop(
        0,
        rounds,
        advance,
        jnp.zeros((attention_lane_count, LANE_FEATURES, LANE_FEATURES), jnp.float32),
    )
    current = incoming
    start_states = []
    for position in range(block_count):
        current = current * carry_keep[position]
        start_states.append(current)
        current = product(current, step_map[position]) + step_add[position]
    stacked = jnp.stack(start_states, axis=0)
    result_lines = output_base + product(queries, flipped(stacked))
    result_lines = jnp.swapaxes(result_lines, 1, 2).reshape(
        row_count, attention_lane_count, LANE_FEATURES
    )
    return ending_result(
        result_lines,
        acceptor_lines,
        adjusted_address,
        payload_entries,
        extra_reward_coefs,
        cluster_normalize_multiplier,
    )


PAIR = 2 * LANE_FEATURES
UNROLL = 4


def split(array):
    high = array.astype(jnp.bfloat16)
    low = (array - high.astype(jnp.float32)).astype(jnp.bfloat16)
    return high, low


def contract(left, right, left_dim, right_dim):
    dims = (((left_dim,), (right_dim,)), ((), ()))
    dot = functools.partial(
        lax.dot_general, dimension_numbers=dims, preferred_element_type=jnp.float32
    )
    wide_left = jnp.concatenate(left, axis=left_dim)
    wide_right = jnp.concatenate([right[0], right[0]], axis=right_dim)
    return dot(wide_left, wide_right) + dot(left[0], right[1])


def mm(left, right):
    return contract(left, right, 1, 0)


def mm_nt(left, right):
    return contract(left, right, 1, 1)


def mm_tn(left, right):
    return contract(left, right, 0, 0)


def mixing_kernel(
    keep_ref,
    recept_ref,
    keyed_ref,
    value_ref,
    decay_ref,
    icl_ref,
    params_ref,
    out_ref,
    state_ref,
):
    step = pl.program_id(1)

    @pl.when(step == 0)
    def _():
        state_ref[...] = jnp.zeros_like(state_ref)

    def iota(shape, dim):
        return lax.broadcasted_iota(jnp.int32, shape, dim)

    square = (PAIR, PAIR)
    row, col = iota(square, 0), iota(square, 1)
    same_head = row // LANE_FEATURES == col // LANE_FEATURES
    ones_head = jnp.where(same_head, 1.0, 0.0).astype(jnp.bfloat16)
    first_head = iota((SPAN, PAIR), 1) < LANE_FEATURES
    strict = row > col
    on_or_below = row >= col
    eye = jnp.where(row == col, 1.0, 0.0)
    triangle = jnp.where(iota((SPAN, SPAN), 0) >= iota((SPAN, SPAN), 1), 1.0, 0.0).astype(
        jnp.bfloat16
    )

    def head_sum(array):
        high, low = split(array)
        return jnp.dot(high, ones_head, preferred_element_type=jnp.float32) + jnp.dot(
            low, ones_head, preferred_element_type=jnp.float32
        )

    def running_sum(array):
        high, low = split(array)
        rest = (array - high.astype(jnp.float32) - low.astype(jnp.float32)).astype(jnp.bfloat16)
        dot = functools.partial(jnp.dot, preferred_element_type=jnp.float32)
        return dot(triangle, high) + (dot(triangle, low) + dot(triangle, rest))

    def stack(array):
        zero = jnp.zeros_like(array)
        return jnp.concatenate(
            [jnp.where(first_head, array, zero), jnp.where(first_head, zero, array)], axis=0
        )

    def param(index):
        return params_ref[index : index + 1, :]

    before_unit, strength, reward, gain = param(0), param(1), param(2), param(3)
    recept, keyed, value = recept_ref[...], keyed_ref[...], value_ref[...]
    log_decay = -decay_limit * jax.nn.sigmoid(decay_ref[...])
    icl = jax.nn.sigmoid(icl_ref[...])
    scaled = keyed * before_unit
    unit_key = scaled / jnp.sqrt(head_sum(scaled * scaled) + norm_eps)
    key_mod = keyed * (1.0 + (icl - 1.0) * strength)
    beta = unit_key * icl
    alpha = -unit_key
    bonus = head_sum(recept * key_mod * reward) * value

    terms = []
    for index in range(recept.shape[0] // SPAN):
        rows = slice(index * SPAN, (index + 1) * SPAN)
        decay_b = log_decay[rows]
        log_sums = running_sum(decay_b)
        decay_in = jnp.exp(log_sums)
        inverse = jnp.exp(-log_sums)
        decay_out = jnp.exp(log_sums[SPAN - 1 :] - log_sums)
        alpha_s = stack(alpha[rows] * jnp.exp(log_sums - decay_b))
        recept_s = stack(recept[rows] * decay_in)
        left = jnp.concatenate([alpha_s, recept_s], axis=0)
        right = jnp.concatenate(
            [stack(beta[rows] * inverse), stack(key_mod[rows] * inverse)], axis=0
        )
        scores = mm_nt(split(left), split(right))
        within = jnp.where(strict, scores[:PAIR, :PAIR], 0.0)
        key_read = jnp.where(strict, scores[:PAIR, PAIR:], 0.0)
        out_beta = jnp.where(on_or_below, scores[PAIR:, :PAIR], 0.0)
        out_key = jnp.where(on_or_below, scores[PAIR:, PAIR:], 0.0)
        value_s = split(stack(value[rows]))
        from_value = mm(split(jnp.concatenate([key_read, out_key], axis=0)), value_s)
        solver = eye
        size = 1
        while size < SPAN:
            pair_mask = jnp.logical_and(
                row // (2 * size) == col // (2 * size), row // size != col // size
            )
            corner = jnp.where(pair_mask, within, 0.0)
            if size == 1:
                solver = solver + corner
            else:
                halves = split(solver)
                solver = solver + mm(halves, split(mm(split(corner), halves)))
            size *= 2
        right_side = jnp.concatenate([alpha_s, from_value[:PAIR]], axis=1)
        reads = mm(split(solver), split(right_side))
        reads_split = split(reads)
        seen = mm(split(out_beta), reads_split)
        queries = recept_s + seen[:, :PAIR]
        base = seen[:, PAIR:] + from_value[PAIR:]
        beta_out = split(stack(beta[rows] * decay_out))
        key_out = split(stack(key_mod[rows] * decay_out))
        moved = mm_tn(reads_split, beta_out)
        step_map = jnp.where(row == col, decay_in[SPAN - 1 :], 0.0) + moved[:PAIR]
        step_add = moved[PAIR:] + mm_tn(value_s, key_out)
        terms.append((split(queries), base, split(step_map), step_add))

    state = state_ref[...]
    results = []
    for index, (queries, base, step_map, step_add) in enumerate(terms):
        state = split(state * keep_ref[step * len(terms) + index])
        result = base + mm_nt(queries, state)
        results.append(result[:SPAN] + result[SPAN:])
        state = mm(state, step_map) + step_add
    state_ref[...] = state

    lines = jnp.concatenate(results, axis=0)
    centered = lines - head_sum(lines) * (1.0 / LANE_FEATURES)
    spread = head_sum(centered * centered) * (1.0 / LANE_FEATURES)
    out_ref[...] = (centered / jnp.sqrt(spread + norm_eps) * gain + bonus).astype(jnp.bfloat16)


def mixed_heads(keep, recept, keyed, value, decay_in, icl_in, params):
    row_count, columns = recept.shape
    block_count = row_count // SPAN
    unroll = UNROLL if block_count % UNROLL == 0 else 1
    rows = unroll * SPAN
    line = pl.BlockSpec((rows, PAIR), lambda pair, step: (step, pair))
    return pl.pallas_call(
        mixing_kernel,
        grid=(columns // PAIR, block_count // unroll),
        in_specs=[pl.BlockSpec(memory_space=pltpu.SMEM)]
        + [line] * 5
        + [pl.BlockSpec((params.shape[0], PAIR), lambda pair, step: (0, pair))],
        out_specs=line,
        out_shape=jax.ShapeDtypeStruct((row_count, columns), jnp.bfloat16),
        scratch_shapes=[pltpu.VMEM((PAIR, PAIR), jnp.float32)],
    )(keep, recept, keyed, value, decay_in, icl_in, params)


def by_heads(
    packed_inputs_slab,
    lagged_blend_coefs,
    acceptor_projector,
    address_projector,
    payload_projector,
    fading_offset_entry,
    fading_left_matrix,
    fading_right_matrix,
    learning_rate_offset,
    learning_left_matrix,
    learning_right_matrix,
    address_before_unitize,
    address_learning_strength,
    extra_reward_coefs,
    cluster_normalize_multiplier,
    paper_spans_sizes,
):
    seq_count = lax.axis_size("seq")
    columns = acceptor_projector.shape[1] // seq_count
    start = lax.axis_index("seq") * columns

    def mine(array):
        return lax.dynamic_slice_in_dim(array, start, columns, axis=array.ndim - 1)

    gathered = lax.all_gather(packed_inputs_slab, ("seq", "head"), axis=0, tiled=True)
    own_recept, own_key, own_value = [
        lax.all_to_all(array, "seq", 1, 0, tiled=True)
        for array in (acceptor_projector, address_projector, payload_projector)
    ]
    row_count = gathered.shape[0]
    block_count = row_count // SPAN
    doc_starts = jnp.cumsum(paper_spans_sizes) - paper_spans_sizes
    span_ids = jnp.arange(block_count, dtype=jnp.int32)
    resets = jnp.any(doc_starts[None, :] == span_ids[:, None], axis=1)
    row_start = jnp.logical_and(jnp.arange(row_count) % SPAN == 0, jnp.repeat(resets, SPAN))
    earlier = jnp.concatenate([jnp.zeros_like(gathered[:1]), gathered[:-1]], axis=0)
    earlier = jnp.where(row_start[:, None], jnp.zeros_like(earlier), earlier)
    x_recept, x_decay, x_key, x_value, x_icl = mixed_inputs(gathered, earlier, lagged_blend_coefs)

    def dot(left, right):
        return jnp.dot(left, right, preferred_element_type=jnp.float32)

    recept = dot(x_recept, own_recept)
    keyed = dot(x_key, own_key)
    value = dot(x_value, own_value)
    decay_low = jnp.tanh(dot(x_decay, fading_left_matrix)).astype(jnp.bfloat16)
    icl_low = dot(x_icl, learning_left_matrix).astype(jnp.bfloat16)
    decay_in = mine(fading_offset_entry) + dot(decay_low, mine(fading_right_matrix))
    icl_in = mine(learning_rate_offset) + dot(icl_low, mine(learning_right_matrix))
    params = jnp.stack(
        [
            mine(array)
            for array in (
                address_before_unitize,
                address_learning_strength,
                extra_reward_coefs,
                cluster_normalize_multiplier,
            )
        ]
    )
    keep = 1.0 - resets.astype(jnp.float32)
    lines = mixed_heads(keep, recept, keyed, value, decay_in, icl_in, params)
    return lax.all_to_all(lines, "seq", 0, 1, tiled=True)


def solution(mesh):
    placed = (
        P(("seq", "head"), None),
        P(),
        P("seq", "head"),
        P("seq", "head"),
        P("seq", "head"),
        P("head"),
        P(),
        P(None, "head"),
        P("head"),
        P(),
        P(None, "head"),
        P("head"),
        P("head"),
        P("head"),
        P("head"),
        P(),
    )

    def run(*arrays):
        width = arrays[2].shape[1] // mesh.shape["head"]
        whole_pairs = width % (mesh.shape["seq"] * PAIR) == 0
        return jax.shard_map(
            by_heads if whole_pairs else per_device,
            mesh=mesh,
            in_specs=placed,
            out_specs=P("seq", "head"),
            check_vma=False,
        )(*arrays)

    return run
```

```python
import functools

import jax
import jax.numpy as jnp
from jax import lax
from jax.experimental import pallas as pl
from jax.experimental.pallas import tpu as pltpu
from jax.sharding import PartitionSpec as P

LANE_FEATURES = 64
SPAN = 64


exact_precision = lax.Precision.HIGHEST
norm_eps = 1e-05
decay_limit = 0.606531


def passed_along(block, axis, distance):
    devices = range(lax.axis_size(axis))
    route = [(i - distance, i) for i in devices if i - distance in devices]
    return lax.ppermute(block, axis, route)


def product(left, right):
    return jnp.matmul(left, right, precision=exact_precision)


def flipped(matrix):
    return jnp.swapaxes(matrix, -1, -2)


def mixed_inputs(packed_inputs_slab, earlier, lagged_blend_coefs):
    current = packed_inputs_slab.astype(jnp.float32)
    change = earlier.astype(jnp.float32) - current
    return [
        (current + change * lagged_blend_coefs[member]).astype(jnp.bfloat16) for member in range(5)
    ]


def prepare(
    acceptor_lines,
    keyed,
    payload_entries,
    x_decay,
    x_icl,
    fading_offset_entry,
    fading_left_matrix,
    fading_right_matrix,
    learning_rate_offset,
    learning_left_matrix,
    learning_right_matrix,
    address_before_unitize,
    address_learning_strength,
):
    decay_low = jnp.tanh(
        jnp.dot(x_decay, fading_left_matrix, preferred_element_type=jnp.float32)
    ).astype(jnp.bfloat16)
    log_decay = -decay_limit * jax.nn.sigmoid(
        fading_offset_entry
        + jnp.dot(decay_low, fading_right_matrix, preferred_element_type=jnp.float32)
    )
    icl_low = jnp.dot(x_icl, learning_left_matrix, preferred_element_type=jnp.float32).astype(
        jnp.bfloat16
    )
    icl = jax.nn.sigmoid(
        learning_rate_offset
        + jnp.dot(icl_low, learning_right_matrix, preferred_element_type=jnp.float32)
    )
    row_count = acceptor_lines.shape[0]
    attention_lane_count = acceptor_lines.shape[1] // LANE_FEATURES
    head_shape = (row_count, attention_lane_count, LANE_FEATURES)
    scaled = (keyed * address_before_unitize).reshape(head_shape)
    unit_key = scaled / jnp.sqrt(jnp.sum(scaled * scaled, axis=-1, keepdims=True) + norm_eps)
    icl_heads = icl.reshape(head_shape)
    adjusted_address = keyed.reshape(head_shape) * (
        1.0
        + (icl_heads - 1.0) * address_learning_strength.reshape(attention_lane_count, LANE_FEATURES)
    )
    return (
        acceptor_lines.reshape(head_shape),
        adjusted_address,
        payload_entries.reshape(head_shape),
        log_decay.reshape(head_shape),
        -unit_key,
        unit_key * icl_heads,
    )


def ending_result(
    result_lines,
    acceptor_lines,
    adjusted_address,
    payload_entries,
    extra_reward_coefs,
    cluster_normalize_multiplier,
):
    attention_lane_count = result_lines.shape[1]
    average = jnp.mean(result_lines, axis=-1, keepdims=True)
    centered = result_lines - average
    spread = jnp.mean(centered * centered, axis=-1, keepdims=True)
    unitized_result = (
        centered
        / jnp.sqrt(spread + norm_eps)
        * cluster_normalize_multiplier.reshape(attention_lane_count, LANE_FEATURES)
    )
    present_reward = (
        jnp.sum(
            acceptor_lines
            * adjusted_address
            * extra_reward_coefs.reshape(attention_lane_count, LANE_FEATURES),
            axis=-1,
            keepdims=True,
        )
        * payload_entries
    )
    return (
        (unitized_result + present_reward).reshape(result_lines.shape[0], -1).astype(jnp.bfloat16)
    )


def span_terms(log_decay, acceptor_lines, keyed, alpha, beta):
    length = log_decay.shape[-2]
    log_sums = jnp.cumsum(log_decay, axis=-2)
    decay_in = jnp.exp(log_sums)
    decay_before = jnp.exp(log_sums - log_decay)
    inverse = jnp.exp(-log_sums)
    decay_out = jnp.exp(log_sums[..., -1:, :] - log_sums)
    alpha_dec = alpha * decay_before
    recept_dec = acceptor_lines * decay_in
    beta_inv = beta * inverse
    key_inv = keyed * inverse
    row_index = lax.broadcasted_iota(jnp.int32, (length, length), 0)
    col_index = lax.broadcasted_iota(jnp.int32, (length, length), 1)
    strict = row_index > col_index
    on_or_below = row_index >= col_index
    solve_matrix = jnp.eye(length, dtype=jnp.float32) - jnp.where(
        strict, product(alpha_dec, flipped(beta_inv)), 0.0
    )
    key_read = jnp.where(strict, product(alpha_dec, flipped(key_inv)), 0.0)
    out_beta = jnp.where(on_or_below, product(recept_dec, flipped(beta_inv)), 0.0)
    out_key = jnp.where(on_or_below, product(recept_dec, flipped(key_inv)), 0.0)
    return (
        solve_matrix,
        key_read,
        out_beta,
        out_key,
        alpha_dec,
        recept_dec,
        decay_in[..., -1, :],
        decay_out,
    )


def per_device(
    packed_inputs_slab,
    lagged_blend_coefs,
    acceptor_projector,
    address_projector,
    payload_projector,
    fading_offset_entry,
    fading_left_matrix,
    fading_right_matrix,
    learning_rate_offset,
    learning_left_matrix,
    learning_right_matrix,
    address_before_unitize,
    address_learning_strength,
    extra_reward_coefs,
    cluster_normalize_multiplier,
    paper_spans_sizes,
):
    gathered = lax.all_gather(packed_inputs_slab, "head", axis=0, tiled=True)
    row_count = gathered.shape[0]
    block_count = row_count // SPAN
    doc_starts = jnp.cumsum(paper_spans_sizes) - paper_spans_sizes
    span_ids = lax.axis_index("seq") * block_count + jnp.arange(block_count, dtype=jnp.int32)
    resets = jnp.any(doc_starts[None, :] == span_ids[:, None], axis=1)
    edge_token = passed_along(gathered[-1:], "seq", 1)
    earlier = jnp.concatenate([edge_token, gathered[:-1]], axis=0)
    row_start = jnp.logical_and(jnp.arange(row_count) % SPAN == 0, jnp.repeat(resets, SPAN))
    earlier = jnp.where(row_start[:, None], jnp.zeros_like(earlier), earlier)
    x_recept, x_decay, x_key, x_value, x_icl = mixed_inputs(gathered, earlier, lagged_blend_coefs)
    whole_recept = lax.all_gather(acceptor_projector, "seq", axis=0, tiled=True)
    whole_key = lax.all_gather(address_projector, "seq", axis=0, tiled=True)
    whole_value = lax.all_gather(payload_projector, "seq", axis=0, tiled=True)
    acceptor_lines = jnp.dot(x_recept, whole_recept, preferred_element_type=jnp.float32)
    keyed = jnp.dot(x_key, whole_key, preferred_element_type=jnp.float32)
    payload_entries = jnp.dot(x_value, whole_value, preferred_element_type=jnp.float32)
    acceptor_lines, adjusted_address, payload_entries, log_decay, alpha, beta = prepare(
        acceptor_lines,
        keyed,
        payload_entries,
        x_decay,
        x_icl,
        fading_offset_entry,
        fading_left_matrix,
        fading_right_matrix,
        learning_rate_offset,
        learning_left_matrix,
        learning_right_matrix,
        address_before_unitize,
        address_learning_strength,
    )
    attention_lane_count = acceptor_lines.shape[1]

    def blocks(array):
        return jnp.swapaxes(
            array.reshape(block_count, SPAN, attention_lane_count, LANE_FEATURES), 1, 2
        )

    recept_b, key_b, value_b, decay_b, alpha_b, beta_b = [
        blocks(array)
        for array in (acceptor_lines, adjusted_address, payload_entries, log_decay, alpha, beta)
    ]
    solve_matrix, key_read, out_beta, out_key, alpha_dec, recept_dec, decay_last, decay_out = (
        span_terms(decay_b, recept_b, key_b, alpha_b, beta_b)
    )
    right_side = jnp.concatenate([alpha_dec, product(key_read, value_b)], axis=-1)
    solved = jax.scipy.linalg.solve_triangular(
        solve_matrix, right_side, lower=True, unit_diagonal=True
    )
    linear_reads = solved[..., :LANE_FEATURES]
    offset_reads = solved[..., LANE_FEATURES:]
    queries = recept_dec + product(out_beta, linear_reads)
    output_base = product(out_beta, offset_reads) + product(out_key, value_b)
    beta_out = beta_b * decay_out
    identity = jnp.eye(LANE_FEATURES, dtype=jnp.float32)
    step_map = identity * decay_last[..., None, :] + product(flipped(linear_reads), beta_out)
    step_add = product(flipped(offset_reads), beta_out) + product(
        flipped(value_b), key_b * decay_out
    )
    carry_keep = 1.0 - resets.astype(jnp.float32)
    device_map = jnp.broadcast_to(identity, (attention_lane_count, LANE_FEATURES, LANE_FEATURES))
    device_add = jnp.zeros((attention_lane_count, LANE_FEATURES, LANE_FEATURES), jnp.float32)
    for position in range(block_count):
        masked = step_map[position] * carry_keep[position]
        device_map = product(device_map, masked)
        device_add = product(device_add, masked) + step_add[position]
    seq_count = lax.axis_size("seq")
    longest = seq_count * block_count // 2
    rounds = min(seq_count - 1, (longest + block_count - 2) // block_count)

    def advance(rounds_done, arriving):
        leaving = product(arriving, device_map) + device_add
        return passed_along(leaving, "seq", 1)

    incoming = lax.fori_loop(
        0,
        rounds,
        advance,
        jnp.zeros((attention_lane_count, LANE_FEATURES, LANE_FEATURES), jnp.float32),
    )
    current = incoming
    start_states = []
    for position in range(block_count):
        current = current * carry_keep[position]
        start_states.append(current)
        current = product(current, step_map[position]) + step_add[position]
    stacked = jnp.stack(start_states, axis=0)
    result_lines = output_base + product(queries, flipped(stacked))
    result_lines = jnp.swapaxes(result_lines, 1, 2).reshape(
        row_count, attention_lane_count, LANE_FEATURES
    )
    return ending_result(
        result_lines,
        acceptor_lines,
        adjusted_address,
        payload_entries,
        extra_reward_coefs,
        cluster_normalize_multiplier,
    )


PAIR = 2 * LANE_FEATURES
UNROLL = 4


def split(array):
    high = array.astype(jnp.bfloat16)
    low = (array - high.astype(jnp.float32)).astype(jnp.bfloat16)
    return high, low


def contract(left, right, left_dim, right_dim):
    dims = (((left_dim,), (right_dim,)), ((), ()))
    dot = functools.partial(
        lax.dot_general, dimension_numbers=dims, preferred_element_type=jnp.float32
    )
    wide_left = jnp.concatenate(left, axis=left_dim)
    wide_right = jnp.concatenate([right[0], right[0]], axis=right_dim)
    return dot(wide_left, wide_right) + dot(left[0], right[1])


def mm(left, right):
    return contract(left, right, 1, 0)


def mm_once(left, right):
    return jnp.dot(
        left.astype(jnp.bfloat16), right.astype(jnp.bfloat16), preferred_element_type=jnp.float32
    )


def mm_nt(left, right):
    return contract(left, right, 1, 1)


def mm_tn(left, right):
    return contract(left, right, 0, 0)


def mixing_kernel(
    keep_ref,
    recept_ref,
    keyed_ref,
    value_ref,
    decay_ref,
    icl_ref,
    params_ref,
    out_ref,
    state_ref,
):
    step = pl.program_id(1)

    @pl.when(step == 0)
    def _():
        state_ref[...] = jnp.zeros_like(state_ref)

    def iota(shape, dim):
        return lax.broadcasted_iota(jnp.int32, shape, dim)

    square = (PAIR, PAIR)
    row, col = iota(square, 0), iota(square, 1)
    same_head = row // LANE_FEATURES == col // LANE_FEATURES
    ones_head = jnp.where(same_head, 1.0, 0.0).astype(jnp.bfloat16)
    first_head = iota((SPAN, PAIR), 1) < LANE_FEATURES
    strict = row > col
    on_or_below = row >= col
    eye = jnp.where(row == col, 1.0, 0.0)
    triangle = jnp.where(iota((SPAN, SPAN), 0) >= iota((SPAN, SPAN), 1), 1.0, 0.0).astype(
        jnp.bfloat16
    )

    def head_sum(array):
        high, low = split(array)
        return jnp.dot(high, ones_head, preferred_element_type=jnp.float32) + jnp.dot(
            low, ones_head, preferred_element_type=jnp.float32
        )

    def running_sum(array):
        high, low = split(array)
        rest = (array - high.astype(jnp.float32) - low.astype(jnp.float32)).astype(jnp.bfloat16)
        dot = functools.partial(jnp.dot, preferred_element_type=jnp.float32)
        return dot(triangle, high) + (dot(triangle, low) + dot(triangle, rest))

    def stack(array):
        zero = jnp.zeros_like(array)
        return jnp.concatenate(
            [jnp.where(first_head, array, zero), jnp.where(first_head, zero, array)], axis=0
        )

    def param(index):
        return params_ref[index : index + 1, :]

    before_unit, strength, reward, gain = param(0), param(1), param(2), param(3)
    recept, keyed, value = recept_ref[...], keyed_ref[...], value_ref[...]
    log_decay = -decay_limit * jax.nn.sigmoid(decay_ref[...])
    icl = jax.nn.sigmoid(icl_ref[...])
    scaled = keyed * before_unit
    unit_key = scaled / jnp.sqrt(head_sum(scaled * scaled) + norm_eps)
    key_mod = keyed * (1.0 + (icl - 1.0) * strength)
    beta = unit_key * icl
    alpha = -unit_key
    bonus = head_sum(recept * key_mod * reward) * value

    terms = []
    for index in range(recept.shape[0] // SPAN):
        rows = slice(index * SPAN, (index + 1) * SPAN)
        decay_b = log_decay[rows]
        log_sums = running_sum(decay_b)
        decay_in = jnp.exp(log_sums)
        inverse = jnp.exp(-log_sums)
        decay_out = jnp.exp(log_sums[SPAN - 1 :] - log_sums)
        alpha_s = stack(alpha[rows] * jnp.exp(log_sums - decay_b))
        recept_s = stack(recept[rows] * decay_in)
        left = jnp.concatenate([alpha_s, recept_s], axis=0)
        right = jnp.concatenate(
            [stack(beta[rows] * inverse), stack(key_mod[rows] * inverse)], axis=0
        )
        scores = mm_nt(split(left), split(right))
        within = jnp.where(strict, scores[:PAIR, :PAIR], 0.0)
        key_read = jnp.where(strict, scores[:PAIR, PAIR:], 0.0)
        out_beta = jnp.where(on_or_below, scores[PAIR:, :PAIR], 0.0)
        out_key = jnp.where(on_or_below, scores[PAIR:, PAIR:], 0.0)
        value_s = split(stack(value[rows]))
        from_value = mm_once(jnp.concatenate([key_read, out_key], axis=0), value_s[0])
        solver = eye
        size = 1
        while size < SPAN:
            pair_mask = jnp.logical_and(
                row // (2 * size) == col // (2 * size), row // size != col // size
            )
            corner = jnp.where(pair_mask, within, 0.0)
            if size == 1:
                solver = solver + corner
            else:
                rounded = solver.astype(jnp.bfloat16)
                solver = solver + mm_once(rounded, mm_once(corner, rounded))
            size *= 2
        residual = eye - solver + mm(split(within), split(solver))
        solver = solver + mm_once(solver, residual)
        right_side = jnp.concatenate([alpha_s, from_value[:PAIR]], axis=1)
        reads = mm(split(solver), split(right_side))
        reads_split = split(reads)
        seen = mm_once(out_beta, reads_split[0])
        queries = recept_s + seen[:, :PAIR]
        base = seen[:, PAIR:] + from_value[PAIR:]
        beta_out = split(stack(beta[rows] * decay_out))
        key_out = split(stack(key_mod[rows] * decay_out))
        moved = mm_tn(reads_split, beta_out)
        step_map = jnp.where(row == col, decay_in[SPAN - 1 :], 0.0) + moved[:PAIR]
        step_add = moved[PAIR:] + mm_tn(value_s, key_out)
        terms.append((queries.astype(jnp.bfloat16), base, split(step_map), step_add))

    state = state_ref[...]
    results = []
    for index, (queries, base, step_map, step_add) in enumerate(terms):
        state = split(state * keep_ref[step * len(terms) + index])
        result = base + lax.dot_general(
            queries, state[0], (((1,), (1,)), ((), ())), preferred_element_type=jnp.float32
        )
        results.append(result[:SPAN] + result[SPAN:])
        state = mm(state, step_map) + step_add
    state_ref[...] = state

    lines = jnp.concatenate(results, axis=0)
    centered = lines - head_sum(lines) * (1.0 / LANE_FEATURES)
    spread = head_sum(centered * centered) * (1.0 / LANE_FEATURES)
    out_ref[...] = (centered / jnp.sqrt(spread + norm_eps) * gain + bonus).astype(jnp.bfloat16)


def mixed_heads(keep, recept, keyed, value, decay_in, icl_in, params):
    row_count, columns = recept.shape
    block_count = row_count // SPAN
    unroll = UNROLL if block_count % UNROLL == 0 else 1
    rows = unroll * SPAN
    line = pl.BlockSpec((rows, PAIR), lambda pair, step: (step, pair))
    return pl.pallas_call(
        mixing_kernel,
        grid=(columns // PAIR, block_count // unroll),
        in_specs=[pl.BlockSpec(memory_space=pltpu.SMEM)]
        + [line] * 5
        + [pl.BlockSpec((params.shape[0], PAIR), lambda pair, step: (0, pair))],
        out_specs=line,
        out_shape=jax.ShapeDtypeStruct((row_count, columns), jnp.bfloat16),
        scratch_shapes=[pltpu.VMEM((PAIR, PAIR), jnp.float32)],
    )(keep, recept, keyed, value, decay_in, icl_in, params)


def by_heads(
    packed_inputs_slab,
    lagged_blend_coefs,
    acceptor_projector,
    address_projector,
    payload_projector,
    fading_offset_entry,
    fading_left_matrix,
    fading_right_matrix,
    learning_rate_offset,
    learning_left_matrix,
    learning_right_matrix,
    address_before_unitize,
    address_learning_strength,
    extra_reward_coefs,
    cluster_normalize_multiplier,
    paper_spans_sizes,
):
    seq_count = lax.axis_size("seq")
    columns = acceptor_projector.shape[1] // seq_count
    start = lax.axis_index("seq") * columns

    def mine(array):
        return lax.dynamic_slice_in_dim(array, start, columns, axis=array.ndim - 1)

    gathered = lax.all_gather(packed_inputs_slab, ("seq", "head"), axis=0, tiled=True)
    own_recept, own_key, own_value = [
        lax.all_to_all(array, "seq", 1, 0, tiled=True)
        for array in (acceptor_projector, address_projector, payload_projector)
    ]
    row_count = gathered.shape[0]
    block_count = row_count // SPAN
    doc_starts = jnp.cumsum(paper_spans_sizes) - paper_spans_sizes
    span_ids = jnp.arange(block_count, dtype=jnp.int32)
    resets = jnp.any(doc_starts[None, :] == span_ids[:, None], axis=1)
    row_start = jnp.logical_and(jnp.arange(row_count) % SPAN == 0, jnp.repeat(resets, SPAN))

    def dot(left, right):
        return jnp.dot(left, right, preferred_element_type=jnp.float32)

    maps = [own_recept, fading_left_matrix, own_key, own_value, learning_left_matrix]
    current_maps, earlier_maps = [], []
    for member, matrix in enumerate(maps):
        coefs = lagged_blend_coefs[member][:, None]
        wide = matrix.astype(jnp.float32)
        current_maps.append((wide * (1.0 - coefs)).astype(jnp.bfloat16))
        earlier_maps.append((wide * coefs).astype(jnp.bfloat16))
    products = dot(gathered, jnp.concatenate(current_maps + earlier_maps, axis=1))
    width = products.shape[1] // 2
    moved = jnp.concatenate([jnp.zeros_like(products[:1, width:]), products[:-1, width:]], axis=0)
    mixed = products[:, :width] + jnp.where(row_start[:, None], 0.0, moved)
    ranks = (columns, fading_left_matrix.shape[1], columns, columns)
    ends = [sum(ranks[: count + 1]) for count in range(len(ranks))]
    recept, decay_sum, keyed, value, icl_sum = jnp.split(mixed, ends, axis=1)
    decay_low = jnp.tanh(decay_sum).astype(jnp.bfloat16)
    icl_low = icl_sum.astype(jnp.bfloat16)
    decay_in = mine(fading_offset_entry) + dot(decay_low, mine(fading_right_matrix))
    icl_in = mine(learning_rate_offset) + dot(icl_low, mine(learning_right_matrix))
    params = jnp.stack(
        [
            mine(array)
            for array in (
                address_before_unitize,
                address_learning_strength,
                extra_reward_coefs,
                cluster_normalize_multiplier,
            )
        ]
    )
    keep = 1.0 - resets.astype(jnp.float32)
    lines = mixed_heads(keep, recept, keyed, value, decay_in, icl_in, params)
    return lax.all_to_all(lines, "seq", 0, 1, tiled=True)


def solution(mesh):
    placed = (
        P(("seq", "head"), None),
        P(),
        P("seq", "head"),
        P("seq", "head"),
        P("seq", "head"),
        P("head"),
        P(),
        P(None, "head"),
        P("head"),
        P(),
        P(None, "head"),
        P("head"),
        P("head"),
        P("head"),
        P("head"),
        P(),
    )

    def run(*arrays):
        width = arrays[2].shape[1] // mesh.shape["head"]
        whole_pairs = width % (mesh.shape["seq"] * PAIR) == 0
        return jax.shard_map(
            by_heads if whole_pairs else per_device,
            mesh=mesh,
            in_specs=placed,
            out_specs=P("seq", "head"),
            check_vma=False,
        )(*arrays)

    return run
```

```python
import functools

import jax
import jax.numpy as jnp
from jax import lax
from jax.experimental import pallas as pl
from jax.experimental.pallas import tpu as pltpu
from jax.sharding import PartitionSpec as P

LANE_FEATURES = 64
SPAN = 64


exact_precision = lax.Precision.HIGHEST
norm_eps = 1e-05
decay_limit = 0.606531


def passed_along(block, axis, distance):
    devices = range(lax.axis_size(axis))
    route = [(i - distance, i) for i in devices if i - distance in devices]
    return lax.ppermute(block, axis, route)


def product(left, right):
    return jnp.matmul(left, right, precision=exact_precision)


def flipped(matrix):
    return jnp.swapaxes(matrix, -1, -2)


def mixed_inputs(packed_inputs_slab, earlier, lagged_blend_coefs):
    current = packed_inputs_slab.astype(jnp.float32)
    change = earlier.astype(jnp.float32) - current
    return [
        (current + change * lagged_blend_coefs[member]).astype(jnp.bfloat16) for member in range(5)
    ]


def prepare(
    acceptor_lines,
    keyed,
    payload_entries,
    x_decay,
    x_icl,
    fading_offset_entry,
    fading_left_matrix,
    fading_right_matrix,
    learning_rate_offset,
    learning_left_matrix,
    learning_right_matrix,
    address_before_unitize,
    address_learning_strength,
):
    decay_low = jnp.tanh(
        jnp.dot(x_decay, fading_left_matrix, preferred_element_type=jnp.float32)
    ).astype(jnp.bfloat16)
    log_decay = -decay_limit * jax.nn.sigmoid(
        fading_offset_entry
        + jnp.dot(decay_low, fading_right_matrix, preferred_element_type=jnp.float32)
    )
    icl_low = jnp.dot(x_icl, learning_left_matrix, preferred_element_type=jnp.float32).astype(
        jnp.bfloat16
    )
    icl = jax.nn.sigmoid(
        learning_rate_offset
        + jnp.dot(icl_low, learning_right_matrix, preferred_element_type=jnp.float32)
    )
    row_count = acceptor_lines.shape[0]
    attention_lane_count = acceptor_lines.shape[1] // LANE_FEATURES
    head_shape = (row_count, attention_lane_count, LANE_FEATURES)
    scaled = (keyed * address_before_unitize).reshape(head_shape)
    unit_key = scaled / jnp.sqrt(jnp.sum(scaled * scaled, axis=-1, keepdims=True) + norm_eps)
    icl_heads = icl.reshape(head_shape)
    adjusted_address = keyed.reshape(head_shape) * (
        1.0
        + (icl_heads - 1.0) * address_learning_strength.reshape(attention_lane_count, LANE_FEATURES)
    )
    return (
        acceptor_lines.reshape(head_shape),
        adjusted_address,
        payload_entries.reshape(head_shape),
        log_decay.reshape(head_shape),
        -unit_key,
        unit_key * icl_heads,
    )


def ending_result(
    result_lines,
    acceptor_lines,
    adjusted_address,
    payload_entries,
    extra_reward_coefs,
    cluster_normalize_multiplier,
):
    attention_lane_count = result_lines.shape[1]
    average = jnp.mean(result_lines, axis=-1, keepdims=True)
    centered = result_lines - average
    spread = jnp.mean(centered * centered, axis=-1, keepdims=True)
    unitized_result = (
        centered
        / jnp.sqrt(spread + norm_eps)
        * cluster_normalize_multiplier.reshape(attention_lane_count, LANE_FEATURES)
    )
    present_reward = (
        jnp.sum(
            acceptor_lines
            * adjusted_address
            * extra_reward_coefs.reshape(attention_lane_count, LANE_FEATURES),
            axis=-1,
            keepdims=True,
        )
        * payload_entries
    )
    return (
        (unitized_result + present_reward).reshape(result_lines.shape[0], -1).astype(jnp.bfloat16)
    )


def span_terms(log_decay, acceptor_lines, keyed, alpha, beta):
    length = log_decay.shape[-2]
    log_sums = jnp.cumsum(log_decay, axis=-2)
    decay_in = jnp.exp(log_sums)
    decay_before = jnp.exp(log_sums - log_decay)
    inverse = jnp.exp(-log_sums)
    decay_out = jnp.exp(log_sums[..., -1:, :] - log_sums)
    alpha_dec = alpha * decay_before
    recept_dec = acceptor_lines * decay_in
    beta_inv = beta * inverse
    key_inv = keyed * inverse
    row_index = lax.broadcasted_iota(jnp.int32, (length, length), 0)
    col_index = lax.broadcasted_iota(jnp.int32, (length, length), 1)
    strict = row_index > col_index
    on_or_below = row_index >= col_index
    solve_matrix = jnp.eye(length, dtype=jnp.float32) - jnp.where(
        strict, product(alpha_dec, flipped(beta_inv)), 0.0
    )
    key_read = jnp.where(strict, product(alpha_dec, flipped(key_inv)), 0.0)
    out_beta = jnp.where(on_or_below, product(recept_dec, flipped(beta_inv)), 0.0)
    out_key = jnp.where(on_or_below, product(recept_dec, flipped(key_inv)), 0.0)
    return (
        solve_matrix,
        key_read,
        out_beta,
        out_key,
        alpha_dec,
        recept_dec,
        decay_in[..., -1, :],
        decay_out,
    )


def per_device(
    packed_inputs_slab,
    lagged_blend_coefs,
    acceptor_projector,
    address_projector,
    payload_projector,
    fading_offset_entry,
    fading_left_matrix,
    fading_right_matrix,
    learning_rate_offset,
    learning_left_matrix,
    learning_right_matrix,
    address_before_unitize,
    address_learning_strength,
    extra_reward_coefs,
    cluster_normalize_multiplier,
    paper_spans_sizes,
):
    gathered = lax.all_gather(packed_inputs_slab, "head", axis=0, tiled=True)
    row_count = gathered.shape[0]
    block_count = row_count // SPAN
    doc_starts = jnp.cumsum(paper_spans_sizes) - paper_spans_sizes
    span_ids = lax.axis_index("seq") * block_count + jnp.arange(block_count, dtype=jnp.int32)
    resets = jnp.any(doc_starts[None, :] == span_ids[:, None], axis=1)
    edge_token = passed_along(gathered[-1:], "seq", 1)
    earlier = jnp.concatenate([edge_token, gathered[:-1]], axis=0)
    row_start = jnp.logical_and(jnp.arange(row_count) % SPAN == 0, jnp.repeat(resets, SPAN))
    earlier = jnp.where(row_start[:, None], jnp.zeros_like(earlier), earlier)
    x_recept, x_decay, x_key, x_value, x_icl = mixed_inputs(gathered, earlier, lagged_blend_coefs)
    whole_recept = lax.all_gather(acceptor_projector, "seq", axis=0, tiled=True)
    whole_key = lax.all_gather(address_projector, "seq", axis=0, tiled=True)
    whole_value = lax.all_gather(payload_projector, "seq", axis=0, tiled=True)
    acceptor_lines = jnp.dot(x_recept, whole_recept, preferred_element_type=jnp.float32)
    keyed = jnp.dot(x_key, whole_key, preferred_element_type=jnp.float32)
    payload_entries = jnp.dot(x_value, whole_value, preferred_element_type=jnp.float32)
    acceptor_lines, adjusted_address, payload_entries, log_decay, alpha, beta = prepare(
        acceptor_lines,
        keyed,
        payload_entries,
        x_decay,
        x_icl,
        fading_offset_entry,
        fading_left_matrix,
        fading_right_matrix,
        learning_rate_offset,
        learning_left_matrix,
        learning_right_matrix,
        address_before_unitize,
        address_learning_strength,
    )
    attention_lane_count = acceptor_lines.shape[1]

    def blocks(array):
        return jnp.swapaxes(
            array.reshape(block_count, SPAN, attention_lane_count, LANE_FEATURES), 1, 2
        )

    recept_b, key_b, value_b, decay_b, alpha_b, beta_b = [
        blocks(array)
        for array in (acceptor_lines, adjusted_address, payload_entries, log_decay, alpha, beta)
    ]
    solve_matrix, key_read, out_beta, out_key, alpha_dec, recept_dec, decay_last, decay_out = (
        span_terms(decay_b, recept_b, key_b, alpha_b, beta_b)
    )
    right_side = jnp.concatenate([alpha_dec, product(key_read, value_b)], axis=-1)
    solved = jax.scipy.linalg.solve_triangular(
        solve_matrix, right_side, lower=True, unit_diagonal=True
    )
    linear_reads = solved[..., :LANE_FEATURES]
    offset_reads = solved[..., LANE_FEATURES:]
    queries = recept_dec + product(out_beta, linear_reads)
    output_base = product(out_beta, offset_reads) + product(out_key, value_b)
    beta_out = beta_b * decay_out
    identity = jnp.eye(LANE_FEATURES, dtype=jnp.float32)
    step_map = identity * decay_last[..., None, :] + product(flipped(linear_reads), beta_out)
    step_add = product(flipped(offset_reads), beta_out) + product(
        flipped(value_b), key_b * decay_out
    )
    carry_keep = 1.0 - resets.astype(jnp.float32)
    device_map = jnp.broadcast_to(identity, (attention_lane_count, LANE_FEATURES, LANE_FEATURES))
    device_add = jnp.zeros((attention_lane_count, LANE_FEATURES, LANE_FEATURES), jnp.float32)
    for position in range(block_count):
        masked = step_map[position] * carry_keep[position]
        device_map = product(device_map, masked)
        device_add = product(device_add, masked) + step_add[position]
    seq_count = lax.axis_size("seq")
    longest = seq_count * block_count // 2
    rounds = min(seq_count - 1, (longest + block_count - 2) // block_count)

    def advance(rounds_done, arriving):
        leaving = product(arriving, device_map) + device_add
        return passed_along(leaving, "seq", 1)

    incoming = lax.fori_loop(
        0,
        rounds,
        advance,
        jnp.zeros((attention_lane_count, LANE_FEATURES, LANE_FEATURES), jnp.float32),
    )
    current = incoming
    start_states = []
    for position in range(block_count):
        current = current * carry_keep[position]
        start_states.append(current)
        current = product(current, step_map[position]) + step_add[position]
    stacked = jnp.stack(start_states, axis=0)
    result_lines = output_base + product(queries, flipped(stacked))
    result_lines = jnp.swapaxes(result_lines, 1, 2).reshape(
        row_count, attention_lane_count, LANE_FEATURES
    )
    return ending_result(
        result_lines,
        acceptor_lines,
        adjusted_address,
        payload_entries,
        extra_reward_coefs,
        cluster_normalize_multiplier,
    )


PAIR = 2 * LANE_FEATURES
UNROLL = 4


def split(array):
    high = array.astype(jnp.bfloat16)
    low = (array - high.astype(jnp.float32)).astype(jnp.bfloat16)
    return high, low


def contract(left, right, left_dim, right_dim):
    dims = (((left_dim,), (right_dim,)), ((), ()))
    dot = functools.partial(
        lax.dot_general, dimension_numbers=dims, preferred_element_type=jnp.float32
    )
    wide_left = jnp.concatenate(left, axis=left_dim)
    wide_right = jnp.concatenate([right[0], right[0]], axis=right_dim)
    return dot(wide_left, wide_right) + dot(left[0], right[1])


def mm(left, right):
    return contract(left, right, 1, 0)


def mm_once(left, right):
    return jnp.dot(
        left.astype(jnp.bfloat16), right.astype(jnp.bfloat16), preferred_element_type=jnp.float32
    )


def mm_nt(left, right):
    return contract(left, right, 1, 1)


def mm_tn(left, right):
    return contract(left, right, 0, 0)


def mixing_kernel(
    keep_ref,
    recept_ref,
    keyed_ref,
    value_ref,
    decay_ref,
    icl_ref,
    params_ref,
    out_ref,
    state_ref,
):
    step = pl.program_id(1)

    @pl.when(step == 0)
    def _():
        state_ref[...] = jnp.zeros_like(state_ref)

    def iota(shape, dim):
        return lax.broadcasted_iota(jnp.int32, shape, dim)

    square = (PAIR, PAIR)
    row, col = iota(square, 0), iota(square, 1)
    same_head = row // LANE_FEATURES == col // LANE_FEATURES
    ones_head = jnp.where(same_head, 1.0, 0.0).astype(jnp.bfloat16)
    first_head = iota((SPAN, PAIR), 1) < LANE_FEATURES
    strict = row > col
    on_or_below = row >= col
    eye = jnp.where(row == col, 1.0, 0.0)
    triangle = jnp.where(iota((SPAN, SPAN), 0) >= iota((SPAN, SPAN), 1), 1.0, 0.0).astype(
        jnp.bfloat16
    )

    def head_sum(array):
        high, low = split(array)
        return jnp.dot(high, ones_head, preferred_element_type=jnp.float32) + jnp.dot(
            low, ones_head, preferred_element_type=jnp.float32
        )

    def running_sum(array):
        high, low = split(array)
        rest = (array - high.astype(jnp.float32) - low.astype(jnp.float32)).astype(jnp.bfloat16)
        dot = functools.partial(jnp.dot, preferred_element_type=jnp.float32)
        return dot(triangle, high) + (dot(triangle, low) + dot(triangle, rest))

    def stack(array):
        zero = jnp.zeros_like(array)
        return jnp.concatenate(
            [jnp.where(first_head, array, zero), jnp.where(first_head, zero, array)], axis=0
        )

    def param(index):
        return params_ref[index : index + 1, :]

    before_unit, strength, reward, gain = param(0), param(1), param(2), param(3)
    recept, keyed, value = recept_ref[...], keyed_ref[...], value_ref[...]
    log_decay = -decay_limit * jax.nn.sigmoid(decay_ref[...])
    icl = jax.nn.sigmoid(icl_ref[...])
    scaled = keyed * before_unit
    unit_key = scaled / jnp.sqrt(head_sum(scaled * scaled) + norm_eps)
    key_mod = keyed * (1.0 + (icl - 1.0) * strength)
    beta = unit_key * icl
    alpha = -unit_key
    bonus = head_sum(recept * key_mod * reward) * value

    group = [slice(at, at + SPAN) for at in range(0, recept.shape[0], SPAN)]

    def each(function, *lists):
        return [function(*items) for items in zip(*lists)]

    decays = [log_decay[rows] for rows in group]
    sums = each(running_sum, decays)
    decay_ins = each(jnp.exp, sums)
    inverses = each(lambda total: jnp.exp(-total), sums)
    decay_outs = each(lambda total: jnp.exp(total[SPAN - 1 :] - total), sums)
    alphas = each(
        lambda rows, total, decay: stack(alpha[rows] * jnp.exp(total - decay)), group, sums, decays
    )
    recepts = each(lambda rows, decay: stack(recept[rows] * decay), group, decay_ins)
    lefts = each(lambda one, two: split(jnp.concatenate([one, two], axis=0)), alphas, recepts)
    rights = each(
        lambda rows, inverse: split(
            jnp.concatenate([stack(beta[rows] * inverse), stack(key_mod[rows] * inverse)], axis=0)
        ),
        group,
        inverses,
    )
    scores = each(mm_nt, lefts, rights)
    withins = [jnp.where(strict, score[:PAIR, :PAIR], 0.0) for score in scores]
    out_betas = [jnp.where(on_or_below, score[PAIR:, :PAIR], 0.0) for score in scores]
    reads_and_outs = [
        jnp.concatenate(
            [
                jnp.where(strict, score[:PAIR, PAIR:], 0.0),
                jnp.where(on_or_below, score[PAIR:, PAIR:], 0.0),
            ],
            axis=0,
        )
        for score in scores
    ]
    values = [split(stack(value[rows])) for rows in group]
    from_values = each(lambda scored, pair: mm_once(scored, pair[0]), reads_and_outs, values)
    solvers = None
    size = 1
    while size < SPAN:
        pair_mask = jnp.logical_and(
            row // (2 * size) == col // (2 * size), row // size != col // size
        )
        corners = [jnp.where(pair_mask, within, 0.0) for within in withins]
        if size == 1:
            solvers = [eye + corner for corner in corners]
        else:
            rounded = [solver.astype(jnp.bfloat16) for solver in solvers]
            inner = each(mm_once, corners, rounded)
            outer = each(mm_once, rounded, inner)
            solvers = each(jnp.add, solvers, outer)
        size *= 2
    checks = each(lambda within, solver: mm(split(within), split(solver)), withins, solvers)
    residuals = each(lambda solver, check: eye - solver + check, solvers, checks)
    fixes = each(mm_once, solvers, residuals)
    solvers = each(lambda solver, fix: split(solver + fix), solvers, fixes)
    right_sides = each(
        lambda one, two: split(jnp.concatenate([one, two[:PAIR]], axis=1)), alphas, from_values
    )
    reads = each(lambda solver, side: split(mm(solver, side)), solvers, right_sides)
    seens = each(lambda out_beta, read: mm_once(out_beta, read[0]), out_betas, reads)
    beta_outs = each(lambda rows, decay: split(stack(beta[rows] * decay)), group, decay_outs)
    key_outs = each(lambda rows, decay: split(stack(key_mod[rows] * decay)), group, decay_outs)
    moves = each(mm_tn, reads, beta_outs)
    adds = each(mm_tn, values, key_outs)
    terms = [
        (
            (recepts[at] + seens[at][:, :PAIR]).astype(jnp.bfloat16),
            seens[at][:, PAIR:] + from_values[at][PAIR:],
            split(jnp.where(row == col, decay_ins[at][SPAN - 1 :], 0.0) + moves[at][:PAIR]),
            moves[at][PAIR:] + adds[at],
        )
        for at in range(len(group))
    ]

    state = state_ref[...]
    results = []
    for index, (queries, base, step_map, step_add) in enumerate(terms):
        state = split(state * keep_ref[step * len(terms) + index])
        result = base + lax.dot_general(
            queries, state[0], (((1,), (1,)), ((), ())), preferred_element_type=jnp.float32
        )
        results.append(result[:SPAN] + result[SPAN:])
        state = mm(state, step_map) + step_add
    state_ref[...] = state

    lines = jnp.concatenate(results, axis=0)
    centered = lines - head_sum(lines) * (1.0 / LANE_FEATURES)
    spread = head_sum(centered * centered) * (1.0 / LANE_FEATURES)
    out_ref[...] = (centered / jnp.sqrt(spread + norm_eps) * gain + bonus).astype(jnp.bfloat16)


def mixed_heads(keep, recept, keyed, value, decay_in, icl_in, params):
    row_count, columns = recept.shape
    block_count = row_count // SPAN
    unroll = UNROLL if block_count % UNROLL == 0 else 1
    rows = unroll * SPAN
    line = pl.BlockSpec((rows, PAIR), lambda pair, step: (step, pair))
    return pl.pallas_call(
        mixing_kernel,
        grid=(columns // PAIR, block_count // unroll),
        in_specs=[pl.BlockSpec(memory_space=pltpu.SMEM)]
        + [line] * 5
        + [pl.BlockSpec((params.shape[0], PAIR), lambda pair, step: (0, pair))],
        out_specs=line,
        out_shape=jax.ShapeDtypeStruct((row_count, columns), jnp.bfloat16),
        scratch_shapes=[pltpu.VMEM((PAIR, PAIR), jnp.float32)],
    )(keep, recept, keyed, value, decay_in, icl_in, params)


CHIP_CORES = 2
SIDE = 2


def exchange_kernel(lines, seq_count, features, first, second, third, whole, own, sems, arrivals, local):
    place, up = lax.axis_index("seq"), lax.axis_index("head")
    layers = seq_count // (SIDE * CHIP_CORES)
    core = lax.rem(place, CHIP_CORES)
    side = lax.rem(place // CHIP_CORES, SIDE)
    far = place // (CHIP_CORES * SIDE)
    other_core, other_side, other_up = 1 - core, 1 - side, 1 - up
    mesh_ids = pl.DeviceIdType.MESH

    def at(far_index, side_index, core_index):
        return (far_index * SIDE + side_index) * CHIP_CORES + core_index

    barrier = pltpu.get_barrier_semaphore()
    side_place = at(far, other_side, core)
    core_place = at(far, side, other_core)
    peers = [lax.rem(place + step, seq_count) for step in range(1, seq_count)]
    for peer in peers:
        pl.semaphore_signal(barrier, inc=1, device_id=(peer, up), device_id_type=mesh_ids)
    pl.semaphore_signal(barrier, inc=1, device_id=(place, other_up), device_id_type=mesh_ids)
    pl.semaphore_wait(barrier, seq_count)

    counter = [0]
    started = []

    def send(source, target, device):
        slot = counter[0]
        counter[0] += 1
        copy = pltpu.make_async_remote_copy(
            src_ref=source,
            dst_ref=target,
            send_sem=sems.at[slot],
            recv_sem=arrivals.at[slot],
            device_id=device,
            device_id_type=mesh_ids,
        )
        copy.start()
        started.append(copy)
        return copy

    def block(seq_index, head_index, start=0, count=lines):
        row = (seq_index * 2 + head_index) * lines + start
        return whole.at[pl.ds(pl.multiple_of(row, 16), count), :]

    mine = block(place, up)
    along = [None]
    for step in range(1, layers):
        along.append(send(features, mine, (at(lax.rem(far + step, layers), side, core), up)))
    to_side, to_up = [], []
    to_side.append(send(features, mine, (side_place, up)))
    to_up.append(send(features, mine, (place, other_up)))
    to_core = [send(features, mine, (core_place, up))]
    kept = pltpu.make_async_copy(features, mine, local.at[0])
    kept.start()

    columns = own.shape[2]
    depth = first.shape[0]
    kept_maps, sent_maps = [], []
    for index, matrix in enumerate((first, second, third)):
        target = own.at[index, pl.ds(pl.multiple_of(place * depth, 16), depth), :]
        for peer in peers:
            source = matrix.at[:, pl.ds(pl.multiple_of(peer * columns, 128), columns)]
            sent_maps.append(send(source, target, (peer, up)))
        source = matrix.at[:, pl.ds(pl.multiple_of(place * columns, 128), columns)]
        kept_maps.append(pltpu.make_async_copy(source, target, local.at[index + 1]))
        kept_maps[-1].start()

    origins = [far] + [lax.rem(far + layers - step, layers) for step in range(1, layers)]
    for step in range(1, layers):
        along[step].wait_recv()
        got = block(at(origins[step], side, core), up)
        to_side.append(send(got, got, (side_place, up)))
        to_up.append(send(got, got, (place, other_up)))
        to_core.append(send(got, got, (core_place, up)))
    half = lines // 2
    corners = []
    for step in range(layers):
        to_side[step].wait_recv()
        source = at(origins[step], other_side, core)
        part = block(source, up, 0, half)
        corner_up = send(part, part, (place, other_up))
        got = block(source, up)
        to_core.append(send(got, got, (core_place, up)))
        to_up[step].wait_recv()
        source = at(origins[step], side, core)
        part = block(source, other_up, half, half)
        corner_side = send(part, part, (side_place, up))
        got = block(source, other_up)
        to_core.append(send(got, got, (core_place, up)))
        corners.append((corner_up, corner_side))
    for step in range(layers):
        for copy in corners[step]:
            copy.wait_recv()
        got = block(at(origins[step], other_side, core), other_up)
        to_core.append(send(got, got, (core_place, up)))
    for copy in to_core:
        copy.wait_recv()
    for copy in sent_maps:
        copy.wait_recv()
    for copy in started:
        copy.wait_send()
    kept.wait()
    for copy in kept_maps:
        copy.wait()


def exchange(features, matrices):
    seq_count = lax.axis_size("seq")
    lines, model = features.shape
    depth, width = matrices[0].shape
    columns = width // seq_count
    layers = seq_count // (SIDE * CHIP_CORES)
    copies = (layers - 1) + 8 * layers + 3 * (seq_count - 1)
    anywhere = pl.BlockSpec(memory_space=pl.ANY)
    return pl.pallas_call(
        functools.partial(exchange_kernel, lines, seq_count),
        in_specs=[anywhere] * 4,
        out_specs=(anywhere, anywhere),
        out_shape=(
            jax.ShapeDtypeStruct((lines * seq_count * 2, model), features.dtype),
            jax.ShapeDtypeStruct((3, depth * seq_count, columns), features.dtype),
        ),
        scratch_shapes=[
            pltpu.SemaphoreType.DMA((copies,)),
            pltpu.SemaphoreType.DMA((copies,)),
            pltpu.SemaphoreType.DMA((4,)),
        ],
        compiler_params=pltpu.CompilerParams(collective_id=0, has_side_effects=True),
    )(features, *matrices)


def by_heads(
    packed_inputs_slab,
    lagged_blend_coefs,
    acceptor_projector,
    address_projector,
    payload_projector,
    fading_offset_entry,
    fading_left_matrix,
    fading_right_matrix,
    learning_rate_offset,
    learning_left_matrix,
    learning_right_matrix,
    address_before_unitize,
    address_learning_strength,
    extra_reward_coefs,
    cluster_normalize_multiplier,
    paper_spans_sizes,
):
    seq_count = lax.axis_size("seq")
    columns = acceptor_projector.shape[1] // seq_count
    start = lax.axis_index("seq") * columns

    def mine(array):
        return lax.dynamic_slice_in_dim(array, start, columns, axis=array.ndim - 1)

    matrices = (acceptor_projector, address_projector, payload_projector)
    if lax.axis_size("head") == 2 and seq_count % (SIDE * CHIP_CORES) == 0:
        gathered, (own_recept, own_key, own_value) = exchange(packed_inputs_slab, matrices)
    else:
        gathered = lax.all_gather(packed_inputs_slab, ("seq", "head"), axis=0, tiled=True)
        own_recept, own_key, own_value = [
            lax.all_to_all(array, "seq", 1, 0, tiled=True) for array in matrices
        ]
    row_count = gathered.shape[0]
    block_count = row_count // SPAN
    doc_starts = jnp.cumsum(paper_spans_sizes) - paper_spans_sizes
    span_ids = jnp.arange(block_count, dtype=jnp.int32)
    resets = jnp.any(doc_starts[None, :] == span_ids[:, None], axis=1)
    row_start = jnp.logical_and(jnp.arange(row_count) % SPAN == 0, jnp.repeat(resets, SPAN))
    earlier = jnp.concatenate([jnp.zeros_like(gathered[:1]), gathered[:-1]], axis=0)
    earlier = jnp.where(row_start[:, None], jnp.zeros_like(earlier), earlier)
    x_recept, x_decay, x_key, x_value, x_icl = mixed_inputs(gathered, earlier, lagged_blend_coefs)

    def dot(left, right):
        return jnp.dot(left, right, preferred_element_type=jnp.float32)

    recept = dot(x_recept, own_recept)
    keyed = dot(x_key, own_key)
    value = dot(x_value, own_value)
    decay_low = jnp.tanh(dot(x_decay, fading_left_matrix)).astype(jnp.bfloat16)
    icl_low = dot(x_icl, learning_left_matrix).astype(jnp.bfloat16)
    decay_in = mine(fading_offset_entry) + dot(decay_low, mine(fading_right_matrix))
    icl_in = mine(learning_rate_offset) + dot(icl_low, mine(learning_right_matrix))
    params = jnp.stack(
        [
            mine(array)
            for array in (
                address_before_unitize,
                address_learning_strength,
                extra_reward_coefs,
                cluster_normalize_multiplier,
            )
        ]
    )
    keep = 1.0 - resets.astype(jnp.float32)
    lines = mixed_heads(keep, recept, keyed, value, decay_in, icl_in, params)
    return lax.all_to_all(lines, "seq", 0, 1, tiled=True)


def solution(mesh):
    placed = (
        P(("seq", "head"), None),
        P(),
        P("seq", "head"),
        P("seq", "head"),
        P("seq", "head"),
        P("head"),
        P(),
        P(None, "head"),
        P("head"),
        P(),
        P(None, "head"),
        P("head"),
        P("head"),
        P("head"),
        P("head"),
        P(),
    )

    def run(*arrays):
        width = arrays[2].shape[1] // mesh.shape["head"]
        whole_pairs = width % (mesh.shape["seq"] * PAIR) == 0
        return jax.shard_map(
            by_heads if whole_pairs else per_device,
            mesh=mesh,
            in_specs=placed,
            out_specs=P("seq", "head"),
            check_vma=False,
        )(*arrays)

    return run
```
